256 devices in a mesh: blk: 256 (over x, z, y, core).
Axes of the slice: x: 4, y: 4, z: 8, core: 2. Of those that a mesh axis runs over, the one named last changes fastest.
Arguments:
- query_states: bfloat16 [65536, 4096], P('blk'), may hold values from -6 to 6
- rotated_key_state: bfloat16 [65536, 1024], P('blk'), may hold values from -6 to 6
- value_state_rows: bfloat16 [65536, 1024], P('blk'), may hold values from -6 to 6
- positions: int32 [65536], P('blk'), may hold values from 0 to 1535, as said below
- residual: bfloat16 [65536, 4096], P('blk'), may hold values from -6 to 6
- norm_gain: float32 [4096], replicated, may hold values from 0.1 to 1.9
- gate_weight: bfloat16 [14336, 4096], P('blk'), may hold values from -0.09375 to 0.09375
- up_weight: bfloat16 [14336, 4096], P('blk'), may hold values from -0.09375 to 0.09375
- down_weight: bfloat16 [14336, 4096], P('blk'), may hold values from -0.375 to 0.375
Outputs:
- attended: bfloat16 [65536, 4096], P('blk')
- ffn_part: bfloat16 [65536, 4096], P('blk')
The draws below stay inside these ranges and needn't reach their ends.
Inputs may be any that keep to these rules, and one draw needn't show every extreme that they name: positions[0] is 0 and every later entry is 0 or one more than the entry before it.
All inputs are finite; a program needn't handle non-finite values.
Results may differ from the reference program's by a relative error of at most 0.0065.
Values may be sent and summed in bfloat16 or wider, within the bound.
No kernel may reach another device: no remote copies, remote signals or barrier semaphores. Data moves between devices by JAX's collectives and lax.ppermute only.
A program may use at most 64 MiB of HBM per device.

```python
import math
import jax
import jax.numpy as jnp
from jax import lax

D = 4096
FF = 14336
QUERY_HEADS = 32
KEY_VALUE_HEADS = 8
HEAD_SIZE = 128
BLOCK_TOKENS = 256
WINDOW_BLOCKS = 4
FFN_STEPS = 4
SEQUENCE_TOKENS = 65536
DOC_MOST = 1536
N_BLK = 256


def random_noise(key, shape):
    return jnp.clip(jax.random.normal(key, shape, jnp.float32), -6.0, 6.0)


def draw_query_states(key, part):
    base_offset = random_noise(jax.random.fold_in(key, 1), (SEQUENCE_TOKENS, QUERY_HEADS * HEAD_SIZE))
    return base_offset.astype(jnp.bfloat16)


def draw_rotated_key_state(key, part):
    base_offset = random_noise(jax.random.fold_in(key, 2), (SEQUENCE_TOKENS, KEY_VALUE_HEADS * HEAD_SIZE))
    return base_offset.astype(jnp.bfloat16)


def draw_positions(key, part):
    number_blocks = SEQUENCE_TOKENS // BLOCK_TOKENS
    doc_count = 2 * number_blocks + 2
    first_key, another_key = jax.random.split(jax.random.fold_in(key, 3))
    lengths = jax.random.randint(first_key, (doc_count,), BLOCK_TOKENS // 2, DOC_MOST + 1)
    longest = jax.random.randint(another_key, (), 0, SEQUENCE_TOKENS // DOC_MOST)
    lengths = jnp.where(jnp.arange(doc_count) == longest, DOC_MOST, lengths)
    starts = jnp.cumsum(lengths) - lengths
    start_flags = jnp.zeros((SEQUENCE_TOKENS,), jnp.int32).at[starts].set(1, mode='drop')
    indices = jnp.arange(SEQUENCE_TOKENS, dtype=jnp.int32)
    doc_begin = lax.cummax(jnp.where(start_flags > 0, indices, 0), axis=0)
    return (indices - doc_begin).astype(jnp.int32)


def steps_of(own_key, dims, shards, least, largest):
    def one(axis_at, shards_of):
        steps = jax.random.uniform(jax.random.fold_in(jax.random.fold_in(own_key, 6), axis_at), (shards_of,), jnp.float32, least / len(shards), largest / len(shards))
        return jnp.repeat(jnp.exp(steps), dims[axis_at] // shards_of).reshape((-1,) + (1,) * (len(dims) - axis_at - 1))

    factor_of = one(*shards[0])
    for cut in shards[1:]:
        factor_of = factor_of * one(*cut)
    return factor_of


def noise(key, dims, width, reach, cuts=(), kind=jnp.bfloat16):
    drawn = jax.random.normal(key, dims, jnp.float32) * width
    if len(cuts) > 0:
        drawn = steps_of(key, dims, cuts, -0.22, 0.18) * drawn
    return jnp.clip(drawn, min=-reach, max=reach).astype(kind)


def setup_inputs(seed: int = 0) -> dict:
    splits = jax.random.split(jax.random.key(seed), 10)
    query_states = draw_query_states(jax.random.fold_in(splits[9], 71), 0)
    rotated_key_state = draw_rotated_key_state(jax.random.fold_in(splits[9], 71), 0)
    value_state_rows = noise(splits[2], (SEQUENCE_TOKENS, KEY_VALUE_HEADS * HEAD_SIZE), 1.0, 6.0, ((0, 256),))
    positions = draw_positions(jax.random.fold_in(splits[9], 71), 0)
    residual = noise(splits[4], (SEQUENCE_TOKENS, D), 1.0, 6.0, ((0, 256),))
    norm_gain = jnp.clip(1.0 + 0.18 * jax.random.normal(splits[5], (D,), jnp.float32), 0.1, 1.9)
    gate_weight = noise(splits[6], (FF, D), D ** -0.5, 0.09375, ((0, 256),))
    up_weight = noise(splits[7], (FF, D), D ** -0.5, 0.09375, ((0, 256),))
    down_weight = noise(splits[8], (FF, D), (FFN_STEPS * FF // N_BLK) ** -0.5, 0.375, ((0, 256),))
    return dict(query_states=query_states, rotated_key_state=rotated_key_state, value_state_rows=value_state_rows, positions=positions, residual=residual, norm_gain=norm_gain, gate_weight=gate_weight, up_weight=up_weight, down_weight=down_weight)


def reference(query_states, rotated_key_state, value_state_rows, positions, residual, norm_gain, gate_weight, up_weight, down_weight):
    number_blocks = SEQUENCE_TOKENS // BLOCK_TOKENS
    heads_per_group = QUERY_HEADS // KEY_VALUE_HEADS
    shard_rows = FF // number_blocks
    padding_rows = (WINDOW_BLOCKS - 1) * BLOCK_TOKENS
    key_with_padding = jnp.concatenate([jnp.zeros((padding_rows, KEY_VALUE_HEADS * HEAD_SIZE), rotated_key_state.dtype), rotated_key_state], axis=0)
    value_with_padding = jnp.concatenate([jnp.zeros((padding_rows, KEY_VALUE_HEADS * HEAD_SIZE), value_state_rows.dtype), value_state_rows], axis=0)
    gate_shards = gate_weight.reshape(number_blocks, shard_rows, D)
    up_shards = up_weight.reshape(number_blocks, shard_rows, D)
    down_shards = down_weight.reshape(number_blocks, shard_rows, D)
    score_scale = 1.0 / math.sqrt(HEAD_SIZE)
    contract = (((1,), (1,)), ((), ()))

    def one_block(block_index):
        start = (block_index * BLOCK_TOKENS).astype(jnp.int32)
        local_queries = lax.dynamic_slice_in_dim(query_states, start, BLOCK_TOKENS, 0)
        local_keys = lax.dynamic_slice_in_dim(key_with_padding, start, WINDOW_BLOCKS * BLOCK_TOKENS, 0)
        local_values = lax.dynamic_slice_in_dim(value_with_padding, start, WINDOW_BLOCKS * BLOCK_TOKENS, 0)
        positions_here = lax.dynamic_slice_in_dim(positions, start, BLOCK_TOKENS, 0)
        residual_here = lax.dynamic_slice_in_dim(residual, start, BLOCK_TOKENS, 0)
        query_index = start + jnp.arange(BLOCK_TOKENS, dtype=jnp.int32)
        key_index = start - padding_rows + jnp.arange(WINDOW_BLOCKS * BLOCK_TOKENS, dtype=jnp.int32)
        visible = (key_index[None, :] <= query_index[:, None]) & (key_index[None, :] >= (query_index - positions_here)[:, None])
        query_wide_float = local_queries.astype(jnp.float32).reshape(BLOCK_TOKENS, KEY_VALUE_HEADS, heads_per_group, HEAD_SIZE)
        key_wide_float = local_keys.astype(jnp.float32).reshape(WINDOW_BLOCKS * BLOCK_TOKENS, KEY_VALUE_HEADS, HEAD_SIZE)
        value_wide_float = local_values.astype(jnp.float32).reshape(WINDOW_BLOCKS * BLOCK_TOKENS, KEY_VALUE_HEADS, HEAD_SIZE)
        scores = jnp.einsum('tgrd,kgd->grtk', query_wide_float, key_wide_float) * score_scale
        scores = jnp.where(visible[None, None], scores, -jnp.inf)
        row_max = lax.optimization_barrier(jnp.max(scores, axis=-1, keepdims=True))
        weights = jnp.exp(scores - row_max)
        denominator = lax.optimization_barrier(jnp.sum(weights, axis=-1, keepdims=True))
        weights_rounded = lax.optimization_barrier(weights.astype(jnp.bfloat16)).astype(jnp.float32)
        mixed = jnp.einsum('grtk,kgd->grtd', weights_rounded, value_wide_float) / denominator
        attended = jnp.transpose(mixed, (2, 0, 1, 3)).reshape(BLOCK_TOKENS, QUERY_HEADS * HEAD_SIZE).astype(jnp.bfloat16)
        stream = residual_here.astype(jnp.float32) + attended.astype(jnp.float32)
        normed = (stream * lax.rsqrt(lax.optimization_barrier(jnp.mean(stream * stream, axis=-1, keepdims=True)) + 1e-05) * norm_gain).astype(jnp.bfloat16)
        owners = (block_index + jnp.arange(FFN_STEPS, dtype=jnp.int32)) % number_blocks
        gate_rows = jnp.take(gate_shards, owners, axis=0).reshape(FFN_STEPS * shard_rows, D)
        up_rows = jnp.take(up_shards, owners, axis=0).reshape(FFN_STEPS * shard_rows, D)
        down_rows = jnp.take(down_shards, owners, axis=0).reshape(FFN_STEPS * shard_rows, D)
        gate_value = lax.dot_general(normed, gate_rows, contract, preferred_element_type=jnp.float32)
        up_value = lax.dot_general(normed, up_rows, contract, preferred_element_type=jnp.float32)
        hidden = (jax.nn.silu(gate_value) * up_value).astype(jnp.bfloat16)
        ffn_part = jnp.dot(hidden, down_rows, preferred_element_type=jnp.float32).astype(jnp.bfloat16)
        return (attended, ffn_part)
    attended_all, ffn_all = lax.map(one_block, jnp.arange(number_blocks, dtype=jnp.int32))
    return (attended_all.reshape(SEQUENCE_TOKENS, QUERY_HEADS * HEAD_SIZE), ffn_all.reshape(SEQUENCE_TOKENS, D))
```

```python
import functools
import math

import jax
import jax.numpy as jnp
from jax import lax
from jax.experimental import pallas as pl
from jax.experimental.pallas import tpu as pltpu
from jax.sharding import PartitionSpec as P

QUERY_HEADS = 32
KEY_VALUE_HEADS = 8
HEAD_SIZE = 128
WINDOW_BLOCKS = 4
FFN_STEPS = 4
GROUP = QUERY_HEADS // KEY_VALUE_HEADS
UNSEEN = -1e30
EXPONENT = math.log2(math.e) / math.sqrt(HEAD_SIZE)
LANES = 128
NT = (((1,), (1,)), ((), ()))


def to_next(value):
    count = lax.axis_size("blk")
    return lax.ppermute(value, "blk", [(i, i + 1) for i in range(count - 1)])


def to_previous(value):
    count = lax.axis_size("blk")
    return lax.ppermute(value, "blk", [(i, (i - 1) % count) for i in range(count)])


def after(value, done):
    return lax.optimization_barrier((value, done))[0]


def attend_kernel(back, last, *refs):
    q_ref, k_ref, v_ref, position_ref = refs[:4]
    if back > 0:
        stat_ref, sum_ref = refs[4:6]
    bias_ref = refs[-1]
    out = refs[4 if back == 0 else 6 : -1]
    rows = q_ref.shape[0]
    key = lax.broadcasted_iota(jnp.int32, (rows, rows), 0) - back * rows
    query = lax.broadcasted_iota(jnp.int32, (rows, rows), 1)
    seen = key >= query - position_ref[...]
    if back == 0:
        seen = seen & (key <= query)
    bias_ref[...] = jnp.where(seen, 0.0, UNSEEN)

    def group(index, _):
        group_columns = pl.ds(pl.multiple_of(index * HEAD_SIZE, HEAD_SIZE), HEAD_SIZE)
        keys = k_ref[:, group_columns]
        values = v_ref[:, group_columns].T
        for head in range(GROUP):
            columns = pl.ds(pl.multiple_of((index * GROUP + head) * HEAD_SIZE, HEAD_SIZE), HEAD_SIZE)
            features = slice(head * HEAD_SIZE, (head + 1) * HEAD_SIZE)
            for start in range(0, rows, LANES):
                some = slice(start, start + LANES)
                scores = lax.dot_general(
                    keys, q_ref[some, columns], NT, preferred_element_type=jnp.float32
                )
                scores = scores + bias_ref[:, some]
                top = jnp.max(scores, axis=0, keepdims=True)
                if back > 0:
                    top_before = stat_ref[index, head : head + 1, some]
                    top = jnp.maximum(top, top_before)
                weights = jnp.exp2((scores - top) * EXPONENT)
                total = jnp.sum(weights, axis=0, keepdims=True)
                mixed = jnp.dot(values, weights.astype(jnp.bfloat16), preferred_element_type=jnp.float32)
                if back > 0:
                    shrink = jnp.exp2((top_before - top) * EXPONENT)
                    total = total + stat_ref[index, GROUP + head : GROUP + head + 1, some] * shrink
                    mixed = mixed + sum_ref[index, features, some] * shrink
                if last:
                    out[0][some, columns] = (mixed * (1.0 / total)).T.astype(jnp.bfloat16)
                else:
                    out[0][index, head : head + 1, some] = top
                    out[0][index, GROUP + head : GROUP + head + 1, some] = total
                    out[1][index, features, some] = mixed
        return 0

    lax.fori_loop(0, KEY_VALUE_HEADS, group, 0, unroll=4)


def attend(back, last, queries, keys, values, positions, carry=()):
    rows = queries.shape[0]
    if last:
        out_shape = (jax.ShapeDtypeStruct(queries.shape, jnp.bfloat16),)
    else:
        out_shape = (
            jax.ShapeDtypeStruct((KEY_VALUE_HEADS, 2 * GROUP, rows), jnp.float32),
            jax.ShapeDtypeStruct((KEY_VALUE_HEADS, GROUP * HEAD_SIZE, rows), jnp.float32),
        )
    return pl.pallas_call(
        functools.partial(attend_kernel, back, last),
        out_shape=out_shape,
        scratch_shapes=[pltpu.VMEM((rows, rows), jnp.float32)],
        name=f"attend_{back}",
        compiler_params=pltpu.CompilerParams(vmem_limit_bytes=16 << 20),
        cost_estimate=pl.CostEstimate(
            flops=4 * QUERY_HEADS * rows * rows * HEAD_SIZE,
            transcendentals=QUERY_HEADS * rows * rows,
            bytes_accessed=12 << 20,
        ),
    )(queries, keys, values, positions, *carry)


def normed_kernel(attended_ref, residual_ref, gain_ref, out_ref):
    step = 16

    def some(index, _):
        rows = pl.ds(pl.multiple_of(index * step, step), step)
        stream = residual_ref[rows, :].astype(jnp.float32) + attended_ref[rows, :].astype(jnp.float32)
        mean = jnp.mean(stream * stream, axis=-1, keepdims=True)
        out_ref[rows, :] = (stream * lax.rsqrt(mean + 1e-05) * gain_ref[...]).astype(jnp.bfloat16)
        return 0

    lax.fori_loop(0, out_ref.shape[0] // step, some, 0, unroll=2)


def gate_kernel(shards, slot, *refs):
    normed_ref = refs[0]
    weights = refs[1 : 1 + 2 * shards]
    out_ref, lhs_ref = refs[1 + 2 * shards :]
    units = weights[0].shape[0]
    for index, weight in enumerate(weights):
        lhs_ref[index * slot : index * slot + units, :] = weight[...]
        lhs_ref[index * slot + units : (index + 1) * slot, :] = jnp.zeros((slot - units, lhs_ref.shape[1]), lhs_ref.dtype)
    both = lax.dot_general(lhs_ref[...], normed_ref[...], NT, preferred_element_type=jnp.float32)
    for shard in range(shards):
        gate = both[2 * shard * slot : (2 * shard + 1) * slot]
        up = both[(2 * shard + 1) * slot : (2 * shard + 2) * slot]
        out_ref[shard * slot : (shard + 1) * slot, :] = (jax.nn.silu(gate) * up).astype(jnp.bfloat16)


def down_kernel(slot, *refs):
    early_ref, late_ref = refs[:2]
    downs = refs[2 : 2 + FFN_STEPS]
    out_ref, rhs_ref = refs[2 + FFN_STEPS :]
    units = downs[0].shape[0]
    for index, rows in enumerate(downs):
        rhs_ref[index * slot : index * slot + units, :] = rows[...]
        rhs_ref[index * slot + units : (index + 1) * slot, :] = jnp.zeros((slot - units, rhs_ref.shape[1]), rhs_ref.dtype)
    hidden = jnp.concatenate([early_ref[...], late_ref[...]], axis=0).T
    width = 512
    for start in range(0, out_ref.shape[1], width):
        some = slice(start, start + width)
        out_ref[:, some] = jnp.dot(hidden, rhs_ref[:, some], preferred_element_type=jnp.float32).astype(jnp.bfloat16)


def normed_rows(attended, residual, gain):
    rows, features = attended.shape
    return pl.pallas_call(
        normed_kernel,
        out_shape=jax.ShapeDtypeStruct((rows, features), jnp.bfloat16),
        name="norm",
        compiler_params=pltpu.CompilerParams(vmem_limit_bytes=16 << 20),
        cost_estimate=pl.CostEstimate(flops=6 * rows * features, transcendentals=rows, bytes_accessed=6 << 20),
    )(attended, residual, gain)


def gate_up(normed, *weights):
    rows, features = normed.shape
    shards = len(weights) // 2
    units = weights[0].shape[0]
    slot = -(-units // 16) * 16
    return pl.pallas_call(
        functools.partial(gate_kernel, shards, slot),
        out_shape=jax.ShapeDtypeStruct((shards * slot, rows), jnp.bfloat16),
        scratch_shapes=[pltpu.VMEM((2 * shards * slot, features), jnp.bfloat16)],
        name=f"gate_up_{shards}",
        compiler_params=pltpu.CompilerParams(vmem_limit_bytes=16 << 20),
        cost_estimate=pl.CostEstimate(
            flops=4 * shards * rows * features * units,
            transcendentals=shards * rows * units,
            bytes_accessed=2 * shards * units * features * 2 + rows * features * 2,
        ),
    )(normed, *weights)


def down(early, late, downs):
    units, features = downs[0].shape
    rows = early.shape[1]
    slot = late.shape[0]
    return pl.pallas_call(
        functools.partial(down_kernel, slot),
        out_shape=jax.ShapeDtypeStruct((rows, features), jnp.bfloat16),
        scratch_shapes=[pltpu.VMEM((FFN_STEPS * slot, features), jnp.bfloat16)],
        name="down",
        compiler_params=pltpu.CompilerParams(vmem_limit_bytes=16 << 20),
        cost_estimate=pl.CostEstimate(
            flops=2 * FFN_STEPS * rows * features * units,
            transcendentals=0,
            bytes_accessed=4 << 20,
        ),
    )(early, late, *downs)


def per_device(
    query_states,
    rotated_key_state,
    value_state_rows,
    positions,
    residual,
    norm_gain,
    gate_weight,
    up_weight,
    down_weight,
):
    positions = positions[None, :]
    keys = [rotated_key_state]
    values = [value_state_rows]
    gates, ups, downs = [gate_weight], [up_weight], [down_weight]
    keys.append(to_next(keys[0]))
    values.append(to_next(values[0]))
    gates.append(to_previous(gates[0]))
    ups.append(to_previous(ups[0]))
    downs.append(to_previous(downs[0]))

    carry = attend(0, False, query_states, keys[0], values[0], positions)
    keys.append(to_next(after(keys[1], carry[0])))
    gates.append(to_previous(after(gates[1], carry[0])))
    values.append(to_next(after(values[1], carry[0])))
    ups.append(to_previous(after(ups[1], carry[0])))

    carry = attend(1, False, query_states, keys[1], values[1], positions, carry)
    downs.append(to_previous(after(downs[1], carry[0])))
    keys.append(to_next(after(keys[2], carry[0])))
    gates.append(to_previous(after(gates[2], carry[0])))
    values.append(to_next(after(values[2], carry[0])))

    carry = attend(2, False, query_states, keys[2], values[2], positions, carry)
    ups.append(to_previous(after(ups[2], carry[0])))
    downs.append(to_previous(after(downs[2], carry[0])))

    (attended,) = attend(3, True, query_states, keys[3], values[3], positions, carry)
    normed = normed_rows(attended, residual, norm_gain[None, :])
    early = gate_up(normed, gates[0], ups[0], gates[1], ups[1], gates[2], ups[2])
    late = gate_up(normed, gates[3], ups[3])
    ffn_part = down(early, late, downs)
    return (attended, ffn_part)


def solution(mesh):
    rows = P("blk", None)
    in_specs = (rows, rows, rows, P("blk"), rows, P(), rows, rows, rows)
    return jax.shard_map(
        per_device, mesh=mesh, in_specs=in_specs, out_specs=(rows, rows), check_vma=False
    )
```

```python
import functools
import math

import jax
import jax.numpy as jnp
from jax import lax
from jax.experimental import pallas as pl
from jax.experimental.pallas import tpu as pltpu
from jax.sharding import PartitionSpec as P

QUERY_HEADS = 32
KEY_VALUE_HEADS = 8
HEAD_SIZE = 128
WINDOW_BLOCKS = 4
FFN_STEPS = 4
GROUP = QUERY_HEADS // KEY_VALUE_HEADS
UNSEEN = -1e30
EXPONENT = math.log2(math.e) / math.sqrt(HEAD_SIZE)
LANES = 128
NT = (((1,), (1,)), ((), ()))


def to_next(value):
    count = lax.axis_size("blk")
    return lax.ppermute(value, "blk", [(i, (i + 1) % count) for i in range(count)])


def to_previous(value):
    count = lax.axis_size("blk")
    return lax.ppermute(value, "blk", [(i, (i - 1) % count) for i in range(count)])


def after(value, done):
    return lax.optimization_barrier((value, done))[0]


def attend_kernel(back, last, *refs):
    if back == 0:
        q_ref, k_ref, v_ref, position_ref = refs[:4]
        *out, bias_ref = refs[4:]
    else:
        q_ref, k_ref, v_ref, position_ref, stat_ref, sum_ref = refs[:6]
        if last:
            residual_ref, gain_ref, attended_out, normed_ref, bias_ref, attended_ref, semaphores = refs[6:]
        else:
            *out, bias_ref = refs[6:]

    def attended_copy(index):
        wide = GROUP * HEAD_SIZE
        columns = pl.ds(pl.multiple_of(index * wide, wide), wide)
        return pltpu.make_async_copy(attended_ref.at[:, columns], attended_out.at[:, columns], semaphores.at[index])

    rows = q_ref.shape[0]
    key = lax.broadcasted_iota(jnp.int32, (rows, rows), 0) - back * rows
    query = lax.broadcasted_iota(jnp.int32, (rows, rows), 1)
    seen = key >= query - position_ref[...]
    if back == 0:
        seen = seen & (key <= query)
    bias_ref[...] = jnp.where(seen, 0.0, UNSEEN)

    def group(index, _):
        group_columns = pl.ds(pl.multiple_of(index * HEAD_SIZE, HEAD_SIZE), HEAD_SIZE)
        keys = k_ref[:, group_columns]
        values = v_ref[:, group_columns].T
        for head in range(GROUP):
            columns = pl.ds(pl.multiple_of((index * GROUP + head) * HEAD_SIZE, HEAD_SIZE), HEAD_SIZE)
            features = slice(head * HEAD_SIZE, (head + 1) * HEAD_SIZE)
            for start in range(0, rows, LANES):
                some = slice(start, start + LANES)
                scores = lax.dot_general(
                    keys, q_ref[some, columns], NT, preferred_element_type=jnp.float32
                )
                scores = scores + bias_ref[:, some]
                top = jnp.max(scores, axis=0, keepdims=True)
                if back > 0:
                    top_before = stat_ref[index, head : head + 1, some]
                    top = jnp.maximum(top, top_before)
                weights = jnp.exp2((scores - top) * EXPONENT)
                total = jnp.sum(weights, axis=0, keepdims=True)
                mixed = jnp.dot(values, weights.astype(jnp.bfloat16), preferred_element_type=jnp.float32)
                if back > 0:
                    shrink = jnp.exp2((top_before - top) * EXPONENT)
                    total = total + stat_ref[index, GROUP + head : GROUP + head + 1, some] * shrink
                    mixed = mixed + sum_ref[index, features, some] * shrink
                if last:
                    attended_ref[some, columns] = (mixed * (1.0 / total)).T.astype(jnp.bfloat16)
                else:
                    out[0][index, head : head + 1, some] = top
                    out[0][index, GROUP + head : GROUP + head + 1, some] = total
                    out[1][index, features, some] = mixed
        if last:
            attended_copy(index).start()
        return 0

    lax.fori_loop(0, KEY_VALUE_HEADS, group, 0, unroll=4)
    if last:
        normed_rows(attended_ref, residual_ref, gain_ref, normed_ref)
        for index in range(KEY_VALUE_HEADS):
            attended_copy(index).wait()


def attend(back, last, queries, keys, values, positions, carry=()):
    rows = queries.shape[0]
    out_specs = None
    if last:
        out_shape = (jax.ShapeDtypeStruct(queries.shape, jnp.bfloat16),) * 2
        out_specs = (pl.BlockSpec(memory_space=pltpu.HBM), pl.BlockSpec(memory_space=pltpu.VMEM))
    else:
        out_shape = (
            jax.ShapeDtypeStruct((KEY_VALUE_HEADS, 2 * GROUP, rows), jnp.float32),
            jax.ShapeDtypeStruct((KEY_VALUE_HEADS, GROUP * HEAD_SIZE, rows), jnp.float32),
        )
    scratch_shapes = [pltpu.VMEM((rows, rows), jnp.float32)]
    in_specs = [pl.BlockSpec(memory_space=pltpu.VMEM)] * (4 + len(carry))
    if last:
        scratch_shapes += [
            pltpu.VMEM(queries.shape, jnp.bfloat16),
            pltpu.SemaphoreType.DMA((KEY_VALUE_HEADS,)),
        ]
    if out_specs is None:
        out_specs = (pl.BlockSpec(memory_space=pltpu.VMEM),) * len(out_shape)
    return pl.pallas_call(
        functools.partial(attend_kernel, back, last),
        out_shape=out_shape,
        in_specs=in_specs,
        out_specs=out_specs,
        scratch_shapes=scratch_shapes,
        name=f"attend_{back}",
        compiler_params=pltpu.CompilerParams(vmem_limit_bytes=16 << 20),
        cost_estimate=pl.CostEstimate(
            flops=4 * QUERY_HEADS * rows * rows * HEAD_SIZE,
            transcendentals=QUERY_HEADS * rows * rows,
            bytes_accessed=12 << 20,
        ),
    )(queries, keys, values, positions, *carry)


def normed_rows(attended_ref, residual_ref, gain_ref, out_ref):
    step = 16

    def some(index, _):
        rows = pl.ds(pl.multiple_of(index * step, step), step)
        stream = residual_ref[rows, :].astype(jnp.float32) + attended_ref[rows, :].astype(jnp.float32)
        mean = jnp.mean(stream * stream, axis=-1, keepdims=True)
        out_ref[rows, :] = (stream * lax.rsqrt(mean + 1e-05) * gain_ref[...]).astype(jnp.bfloat16)
        return 0

    lax.fori_loop(0, out_ref.shape[0] // step, some, 0, unroll=2)


def gate_kernel(shards, slot, *refs):
    normed_ref = refs[0]
    weights = refs[1 : 1 + 2 * shards]
    out_ref, lhs_ref = refs[1 + 2 * shards :]
    units = weights[0].shape[0]
    for index, weight in enumerate(weights):
        lhs_ref[index * slot : index * slot + units, :] = weight[...]
        lhs_ref[index * slot + units : (index + 1) * slot, :] = jnp.zeros((slot - units, lhs_ref.shape[1]), lhs_ref.dtype)
    both = lax.dot_general(lhs_ref[...], normed_ref[...], NT, preferred_element_type=jnp.float32)
    for shard in range(shards):
        gate = both[2 * shard * slot : (2 * shard + 1) * slot]
        up = both[(2 * shard + 1) * slot : (2 * shard + 2) * slot]
        out_ref[shard * slot : (shard + 1) * slot, :] = (jax.nn.silu(gate) * up).astype(jnp.bfloat16)


def down_kernel(slot, *refs):
    early_ref, late_ref = refs[:2]
    downs = refs[2 : 2 + FFN_STEPS]
    out_ref, rhs_ref, piece_ref, semaphores = refs[2 + FFN_STEPS :]
    units = downs[0].shape[0]
    for index, rows in enumerate(downs):
        rhs_ref[index * slot : index * slot + units, :] = rows[...]
        rhs_ref[index * slot + units : (index + 1) * slot, :] = jnp.zeros((slot - units, rhs_ref.shape[1]), rhs_ref.dtype)
    hidden = jnp.concatenate([early_ref[...], late_ref[...]], axis=0).T
    width = out_ref.shape[1] // semaphores.shape[0]
    copies = []
    for piece in range(semaphores.shape[0]):
        some = slice(piece * width, (piece + 1) * width)
        piece_ref[:, some] = jnp.dot(hidden, rhs_ref[:, some], preferred_element_type=jnp.float32).astype(jnp.bfloat16)
        copies.append(pltpu.make_async_copy(piece_ref.at[:, some], out_ref.at[:, some], semaphores.at[piece]))
        copies[-1].start()
    for copy in copies:
        copy.wait()


def gate_up(normed, *weights):
    rows, features = normed.shape
    shards = len(weights) // 2
    units = weights[0].shape[0]
    slot = -(-units // 16) * 16
    return pl.pallas_call(
        functools.partial(gate_kernel, shards, slot),
        out_shape=jax.ShapeDtypeStruct((shards * slot, rows), jnp.bfloat16),
        scratch_shapes=[pltpu.VMEM((2 * shards * slot, features), jnp.bfloat16)],
        name=f"gate_up_{shards}",
        compiler_params=pltpu.CompilerParams(vmem_limit_bytes=16 << 20),
        cost_estimate=pl.CostEstimate(
            flops=4 * shards * rows * features * units,
            transcendentals=shards * rows * units,
            bytes_accessed=2 * shards * units * features * 2 + rows * features * 2,
        ),
    )(normed, *weights)


def down(early, late, downs):
    units, features = downs[0].shape
    rows = early.shape[1]
    slot = late.shape[0]
    return pl.pallas_call(
        functools.partial(down_kernel, slot),
        out_shape=jax.ShapeDtypeStruct((rows, features), jnp.bfloat16),
        out_specs=pl.BlockSpec(memory_space=pltpu.HBM),
        scratch_shapes=[
            pltpu.VMEM((FFN_STEPS * slot, features), jnp.bfloat16),
            pltpu.VMEM((rows, features), jnp.bfloat16),
            pltpu.SemaphoreType.DMA((8,)),
        ],
        name="down",
        compiler_params=pltpu.CompilerParams(vmem_limit_bytes=16 << 20),
        cost_estimate=pl.CostEstimate(
            flops=64 * 2 * FFN_STEPS * rows * features * units,
            transcendentals=0,
            bytes_accessed=4 << 20,
        ),
    )(early, late, *downs)


def per_device(
    query_states,
    rotated_key_state,
    value_state_rows,
    positions,
    residual,
    norm_gain,
    gate_weight,
    up_weight,
    down_weight,
):
    positions = positions[None, :]
    keys = [rotated_key_state]
    values = [value_state_rows]
    gates, ups, downs = [gate_weight], [up_weight], [down_weight]
    gates.append(to_previous(gates[0]))
    ups.append(to_previous(ups[0]))
    downs.append(to_previous(downs[0]))
    keys.append(to_next(keys[0]))
    values.append(to_next(values[0]))

    carry = attend(0, False, query_states, keys[0], values[0], positions)
    keys.append(to_next(after(keys[1], carry[0])))
    gates.append(to_previous(after(gates[1], carry[0])))
    values.append(to_next(after(values[1], carry[0])))
    ups.append(to_previous(after(ups[1], carry[0])))

    carry = attend(1, False, query_states, keys[1], values[1], positions, carry)
    downs.append(to_previous(after(downs[1], carry[0])))
    keys.append(to_next(after(keys[2], carry[0])))
    gates.append(to_previous(after(gates[2], carry[0])))
    values.append(to_next(after(values[2], carry[0])))

    carry = attend(2, False, query_states, keys[2], values[2], positions, carry)
    ups.append(to_previous(after(ups[2], carry[0])))
    downs.append(to_previous(after(downs[2], carry[0])))

    attended, normed = attend(
        3, True, query_states, keys[3], values[3], positions, (*carry, residual, norm_gain[None, :])
    )
    early = gate_up(normed, gates[0], ups[0], gates[1], ups[1], gates[2], ups[2])
    late = gate_up(normed, gates[3], ups[3])
    ffn_part = down(early, late, downs)
    return (attended, ffn_part)


def solution(mesh):
    rows = P("blk", None)
    in_specs = (rows, rows, rows, P("blk"), rows, P(), rows, rows, rows)
    return jax.shard_map(
        per_device, mesh=mesh, in_specs=in_specs, out_specs=(rows, rows), check_vma=False
    )
```

```python
import functools
import math

import jax
import jax.numpy as jnp
from jax import lax
from jax.experimental import pallas as pl
from jax.experimental.pallas import tpu as pltpu
from jax.sharding import PartitionSpec as P

QUERY_HEADS = 32
KEY_VALUE_HEADS = 8
HEAD_SIZE = 128
WINDOW_BLOCKS = 4
FFN_STEPS = 4
GROUP = QUERY_HEADS // KEY_VALUE_HEADS
UNSEEN = -1e30
EXPONENT = math.log2(math.e) / math.sqrt(HEAD_SIZE)
LANES = 128
CAUSAL_FLOPS = 20 * 10**9
NT = (((1,), (1,)), ((), ()))


def to_next(value):
    count = lax.axis_size("blk")
    return lax.ppermute(value, "blk", [(i, (i + 1) % count) for i in range(count)])


def to_previous(value):
    count = lax.axis_size("blk")
    return lax.ppermute(value, "blk", [(i, (i - 1) % count) for i in range(count)])


def after(value, done):
    return lax.optimization_barrier((value, done))[0]


def attend_kernel(back, last, *refs):
    if back == 0:
        q_ref, k_ref, v_ref, position_ref, causal_ref = refs[:5]
        *out, bias_ref = refs[5:]
    else:
        q_ref, k_ref, v_ref, position_ref, stat_ref, sum_ref = refs[:6]
        if last:
            residual_ref, gain_ref, attended_out, normed_ref, bias_ref, attended_ref, semaphores = refs[6:]
        else:
            *out, bias_ref = refs[6:]

    def attended_copy(index):
        wide = GROUP * HEAD_SIZE
        columns = pl.ds(pl.multiple_of(index * wide, wide), wide)
        return pltpu.make_async_copy(attended_ref.at[:, columns], attended_out.at[:, columns], semaphores.at[index])

    rows = q_ref.shape[0]
    key = lax.broadcasted_iota(jnp.int32, (rows, rows), 0) - back * rows
    query = lax.broadcasted_iota(jnp.int32, (rows, rows), 1)
    seen = key >= query - position_ref[...]
    bias_ref[...] = jnp.where(seen, causal_ref[...] if back == 0 else 0.0, UNSEEN)

    def group(index, _):
        group_columns = pl.ds(pl.multiple_of(index * HEAD_SIZE, HEAD_SIZE), HEAD_SIZE)
        keys = k_ref[:, group_columns]
        values = v_ref[:, group_columns].T
        for head in range(GROUP):
            columns = pl.ds(pl.multiple_of((index * GROUP + head) * HEAD_SIZE, HEAD_SIZE), HEAD_SIZE)
            features = slice(head * HEAD_SIZE, (head + 1) * HEAD_SIZE)
            for start in range(0, rows, LANES):
                some = slice(start, start + LANES)
                scores = lax.dot_general(
                    keys, q_ref[some, columns], NT, preferred_element_type=jnp.float32
                )
                scores = scores + bias_ref[:, some]
                top = jnp.max(scores, axis=0, keepdims=True)
                if back > 0:
                    top_before = stat_ref[index, head : head + 1, some]
                    top = jnp.maximum(top, top_before)
                weights = jnp.exp2((scores - top) * EXPONENT)
                total = jnp.sum(weights, axis=0, keepdims=True)
                mixed = jnp.dot(values, weights.astype(jnp.bfloat16), preferred_element_type=jnp.float32)
                if back > 0:
                    shrink = jnp.exp2((top_before - top) * EXPONENT)
                    total = total + stat_ref[index, GROUP + head : GROUP + head + 1, some] * shrink
                    mixed = mixed + sum_ref[index, features, some] * shrink
                if last:
                    attended_ref[some, columns] = (mixed * (1.0 / total)).T.astype(jnp.bfloat16)
                else:
                    out[0][index, head : head + 1, some] = top
                    out[0][index, GROUP + head : GROUP + head + 1, some] = total
                    out[1][index, features, some] = mixed
        if last:
            attended_copy(index).start()
        return 0

    lax.fori_loop(0, KEY_VALUE_HEADS, group, 0, unroll=4)
    if last:
        normed_rows(attended_ref, residual_ref, gain_ref, normed_ref)
        for index in range(KEY_VALUE_HEADS):
            attended_copy(index).wait()


def attend(back, last, queries, keys, values, positions, carry=()):
    rows = queries.shape[0]
    out_specs = None
    if last:
        out_shape = (jax.ShapeDtypeStruct(queries.shape, jnp.bfloat16),) * 2
        out_specs = (pl.BlockSpec(memory_space=pltpu.HBM), pl.BlockSpec(memory_space=pltpu.VMEM))
    else:
        out_shape = (
            jax.ShapeDtypeStruct((KEY_VALUE_HEADS, 2 * GROUP, rows), jnp.float32),
            jax.ShapeDtypeStruct((KEY_VALUE_HEADS, GROUP * HEAD_SIZE, rows), jnp.float32),
        )
    scratch_shapes = [pltpu.VMEM((rows, rows), jnp.float32)]
    in_specs = [pl.BlockSpec(memory_space=pltpu.VMEM)] * (4 + len(carry))
    if last:
        scratch_shapes += [
            pltpu.VMEM(queries.shape, jnp.bfloat16),
            pltpu.SemaphoreType.DMA((KEY_VALUE_HEADS,)),
        ]
    if out_specs is None:
        out_specs = (pl.BlockSpec(memory_space=pltpu.VMEM),) * len(out_shape)
    return pl.pallas_call(
        functools.partial(attend_kernel, back, last),
        out_shape=out_shape,
        in_specs=in_specs,
        out_specs=out_specs,
        scratch_shapes=scratch_shapes,
        name=f"attend_{back}",
        compiler_params=pltpu.CompilerParams(vmem_limit_bytes=16 << 20),
        cost_estimate=pl.CostEstimate(
            flops=4 * QUERY_HEADS * rows * rows * HEAD_SIZE,
            transcendentals=QUERY_HEADS * rows * rows,
            bytes_accessed=12 << 20,
        ),
    )(queries, keys, values, positions, *carry)


def weigh_kernel(back, q_ref, k_ref, position_ref, stat_ref, weights_out, stat_out, bias_ref):
    rows = q_ref.shape[0]
    key = lax.broadcasted_iota(jnp.int32, (rows, rows), 0) - back * rows
    query = lax.broadcasted_iota(jnp.int32, (rows, rows), 1)
    bias_ref[...] = jnp.where(key >= query - position_ref[...], 0.0, UNSEEN)

    def group(index, _):
        keys = k_ref[:, pl.ds(pl.multiple_of(index * HEAD_SIZE, HEAD_SIZE), HEAD_SIZE)]
        for head in range(GROUP):
            columns = pl.ds(pl.multiple_of((index * GROUP + head) * HEAD_SIZE, HEAD_SIZE), HEAD_SIZE)
            for start in range(0, rows, LANES):
                some = slice(start, start + LANES)
                scores = lax.dot_general(
                    keys, q_ref[some, columns], NT, preferred_element_type=jnp.float32
                )
                scores = scores + bias_ref[:, some]
                top_before = stat_ref[index, head : head + 1, some]
                top = jnp.maximum(jnp.max(scores, axis=0, keepdims=True), top_before)
                weights = jnp.exp2((scores - top) * EXPONENT)
                shrink = jnp.exp2((top_before - top) * EXPONENT)
                total = jnp.sum(weights, axis=0, keepdims=True)
                total = total + stat_ref[index, GROUP + head : GROUP + head + 1, some] * shrink
                weights_out[index, head * rows : (head + 1) * rows, some] = weights.astype(jnp.bfloat16)
                stat_out[index, head : head + 1, some] = shrink / total
                stat_out[index, GROUP + head : GROUP + head + 1, some] = 1.0 / total
        return 0

    lax.fori_loop(0, KEY_VALUE_HEADS, group, 0, unroll=4)


def weigh(back, queries, keys, positions, stat):
    rows = queries.shape[0]
    return pl.pallas_call(
        functools.partial(weigh_kernel, back),
        out_shape=(
            jax.ShapeDtypeStruct((KEY_VALUE_HEADS, GROUP * rows, rows), jnp.bfloat16),
            jax.ShapeDtypeStruct(stat.shape, jnp.float32),
        ),
        scratch_shapes=[pltpu.VMEM((rows, rows), jnp.float32)],
        name=f"weigh_{back}",
        compiler_params=pltpu.CompilerParams(vmem_limit_bytes=16 << 20),
        cost_estimate=pl.CostEstimate(
            flops=2 * QUERY_HEADS * rows * rows * HEAD_SIZE,
            transcendentals=QUERY_HEADS * rows * rows,
            bytes_accessed=8 << 20,
        ),
    )(queries, keys, positions, stat)


def mix_kernel(v_ref, weights_ref, stat_ref, sum_ref, residual_ref, gain_ref, attended_out, normed_ref, attended_ref, semaphores):
    rows = v_ref.shape[0]
    wide = GROUP * HEAD_SIZE

    def attended_copy(index):
        columns = pl.ds(pl.multiple_of(index * wide, wide), wide)
        return pltpu.make_async_copy(attended_ref.at[:, columns], attended_out.at[:, columns], semaphores.at[index])

    def group(index, _):
        values = v_ref[:, pl.ds(pl.multiple_of(index * HEAD_SIZE, HEAD_SIZE), HEAD_SIZE)].T
        for head in range(GROUP):
            columns = pl.ds(pl.multiple_of((index * GROUP + head) * HEAD_SIZE, HEAD_SIZE), HEAD_SIZE)
            features = slice(head * HEAD_SIZE, (head + 1) * HEAD_SIZE)
            for start in range(0, rows, LANES):
                some = slice(start, start + LANES)
                mixed = jnp.dot(
                    values,
                    weights_ref[index, head * rows : (head + 1) * rows, some],
                    preferred_element_type=jnp.float32,
                )
                mixed = mixed * stat_ref[index, GROUP + head : GROUP + head + 1, some]
                mixed = mixed + sum_ref[index, features, some] * stat_ref[index, head : head + 1, some]
                attended_ref[some, columns] = mixed.T.astype(jnp.bfloat16)
        attended_copy(index).start()
        return 0

    lax.fori_loop(0, KEY_VALUE_HEADS, group, 0, unroll=4)
    normed_rows(attended_ref, residual_ref, gain_ref, normed_ref)
    for index in range(KEY_VALUE_HEADS):
        attended_copy(index).wait()


def mix(values, weights, stat, sums, residual, gain):
    return pl.pallas_call(
        mix_kernel,
        out_shape=(jax.ShapeDtypeStruct(residual.shape, jnp.bfloat16),) * 2,
        out_specs=(pl.BlockSpec(memory_space=pltpu.HBM), pl.BlockSpec(memory_space=pltpu.VMEM)),
        scratch_shapes=[
            pltpu.VMEM(residual.shape, jnp.bfloat16),
            pltpu.SemaphoreType.DMA((KEY_VALUE_HEADS,)),
        ],
        name="mix",
        compiler_params=pltpu.CompilerParams(vmem_limit_bytes=16 << 20),
        cost_estimate=pl.CostEstimate(
            flops=2 * weights.size * HEAD_SIZE, transcendentals=0, bytes_accessed=12 << 20
        ),
    )(values, weights, stat, sums, residual, gain)


def causal_kernel(out_ref):
    key = lax.broadcasted_iota(jnp.int32, out_ref.shape, 0)
    query = lax.broadcasted_iota(jnp.int32, out_ref.shape, 1)
    out_ref[...] = jnp.where(key <= query, 0.0, UNSEEN)


def causal_bias(rows):
    return pl.pallas_call(
        causal_kernel,
        out_shape=jax.ShapeDtypeStruct((rows, rows), jnp.float32),
        name="causal",
        compiler_params=pltpu.CompilerParams(vmem_limit_bytes=4 << 20),
        cost_estimate=pl.CostEstimate(flops=CAUSAL_FLOPS, transcendentals=0, bytes_accessed=rows * rows * 4),
    )()


def normed_rows(attended_ref, residual_ref, gain_ref, out_ref):
    step = 16

    def some(index, _):
        rows = pl.ds(pl.multiple_of(index * step, step), step)
        stream = residual_ref[rows, :].astype(jnp.float32) + attended_ref[rows, :].astype(jnp.float32)
        mean = jnp.mean(stream * stream, axis=-1, keepdims=True)
        out_ref[rows, :] = (stream * lax.rsqrt(mean + 1e-05) * gain_ref[...]).astype(jnp.bfloat16)
        return 0

    lax.fori_loop(0, out_ref.shape[0] // step, some, 0, unroll=2)


def gate_kernel(shards, slot, *refs):
    normed_ref = refs[0]
    weights = refs[1 : 1 + 2 * shards]
    out_ref, lhs_ref = refs[1 + 2 * shards :]
    units = weights[0].shape[0]
    for index, weight in enumerate(weights):
        lhs_ref[index * slot : index * slot + units, :] = weight[...]
        lhs_ref[index * slot + units : (index + 1) * slot, :] = jnp.zeros((slot - units, lhs_ref.shape[1]), lhs_ref.dtype)
    both = lax.dot_general(lhs_ref[...], normed_ref[...], NT, preferred_element_type=jnp.float32)
    for shard in range(shards):
        gate = both[2 * shard * slot : (2 * shard + 1) * slot]
        up = both[(2 * shard + 1) * slot : (2 * shard + 2) * slot]
        out_ref[shard * slot : (shard + 1) * slot, :] = (jax.nn.silu(gate) * up).astype(jnp.bfloat16)


def down_kernel(slot, *refs):
    hidden_ref = refs[0]
    downs = refs[1 : 1 + FFN_STEPS]
    out_ref, rhs_ref, piece_ref, semaphores = refs[1 + FFN_STEPS :]
    units = downs[0].shape[0]
    for index, rows in enumerate(downs):
        rhs_ref[index * slot : index * slot + units, :] = rows[...]
        rhs_ref[index * slot + units : (index + 1) * slot, :] = jnp.zeros((slot - units, rhs_ref.shape[1]), rhs_ref.dtype)
    hidden = hidden_ref[...].T
    width = out_ref.shape[1] // semaphores.shape[0]
    copies = []
    for piece in range(semaphores.shape[0]):
        some = slice(piece * width, (piece + 1) * width)
        piece_ref[:, some] = jnp.dot(hidden, rhs_ref[:, some], preferred_element_type=jnp.float32).astype(jnp.bfloat16)
        copies.append(pltpu.make_async_copy(piece_ref.at[:, some], out_ref.at[:, some], semaphores.at[piece]))
        copies[-1].start()
    for copy in copies:
        copy.wait()


def gate_up(normed, *weights):
    rows, features = normed.shape
    shards = len(weights) // 2
    units = weights[0].shape[0]
    slot = -(-units // 16) * 16
    return pl.pallas_call(
        functools.partial(gate_kernel, shards, slot),
        out_shape=jax.ShapeDtypeStruct((shards * slot, rows), jnp.bfloat16),
        scratch_shapes=[pltpu.VMEM((2 * shards * slot, features), jnp.bfloat16)],
        name=f"gate_up_{shards}",
        compiler_params=pltpu.CompilerParams(vmem_limit_bytes=16 << 20),
        cost_estimate=pl.CostEstimate(
            flops=4 * shards * rows * features * units,
            transcendentals=shards * rows * units,
            bytes_accessed=2 * shards * units * features * 2 + rows * features * 2,
        ),
    )(normed, *weights)


def down(hidden, downs):
    units, features = downs[0].shape
    rows = hidden.shape[1]
    slot = hidden.shape[0] // FFN_STEPS
    return pl.pallas_call(
        functools.partial(down_kernel, slot),
        out_shape=jax.ShapeDtypeStruct((rows, features), jnp.bfloat16),
        out_specs=pl.BlockSpec(memory_space=pltpu.HBM),
        scratch_shapes=[
            pltpu.VMEM((FFN_STEPS * slot, features), jnp.bfloat16),
            pltpu.VMEM((rows, features), jnp.bfloat16),
            pltpu.SemaphoreType.DMA((8,)),
        ],
        name="down",
        compiler_params=pltpu.CompilerParams(vmem_limit_bytes=16 << 20),
        cost_estimate=pl.CostEstimate(
            flops=64 * 2 * FFN_STEPS * rows * features * units,
            transcendentals=0,
            bytes_accessed=4 << 20,
        ),
    )(hidden, *downs)


def per_device(
    query_states,
    rotated_key_state,
    value_state_rows,
    positions,
    residual,
    norm_gain,
    gate_weight,
    up_weight,
    down_weight,
):
    positions = positions[None, :]
    keys = [rotated_key_state]
    values = [value_state_rows]
    gates, ups, downs = [gate_weight], [up_weight], [down_weight]
    causal = causal_bias(query_states.shape[0])
    gates.append(to_previous(after(gates[0], causal)))
    ups.append(to_previous(after(ups[0], causal)))
    downs.append(to_previous(after(downs[0], causal)))
    keys.append(to_next(after(keys[0], causal)))
    values.append(to_next(after(values[0], causal)))

    carry = attend(0, False, query_states, keys[0], values[0], positions, (causal,))
    keys.append(to_next(after(keys[1], carry[0])))
    gates.append(to_previous(after(gates[1], carry[0])))
    values.append(to_next(after(values[1], carry[0])))
    ups.append(to_previous(after(ups[1], carry[0])))

    carry = attend(1, False, query_states, keys[1], values[1], positions, carry)
    downs.append(to_previous(after(downs[1], carry[0])))
    keys.append(to_next(after(keys[2], carry[0])))
    gates.append(to_previous(after(gates[2], carry[0])))
    values.append(to_next(after(values[2], carry[0])))

    carry = attend(2, False, query_states, keys[2], values[2], positions, carry)
    ups.append(to_previous(after(ups[2], carry[0])))
    downs.append(to_previous(after(downs[2], carry[0])))

    weights, scales = weigh(3, query_states, keys[3], positions, carry[0])
    attended, normed = mix(values[3], weights, scales, carry[1], residual, norm_gain[None, :])
    units = gate_up(normed, *[rows for pair in zip(gates, ups) for rows in pair])
    ffn_part = down(units, downs)
    return (attended, ffn_part)


def solution(mesh):
    rows = P("blk", None)
    in_specs = (rows, rows, rows, P("blk"), rows, P(), rows, rows, rows)
    return jax.shard_map(
        per_device, mesh=mesh, in_specs=in_specs, out_specs=(rows, rows), check_vma=False
    )
```

```python
import functools
import math

import jax
import jax.numpy as jnp
from jax import lax
from jax.experimental import pallas as pl
from jax.experimental.pallas import tpu as pltpu
from jax.sharding import PartitionSpec as P

QUERY_HEADS = 32
KEY_VALUE_HEADS = 8
HEAD_SIZE = 128
WINDOW_BLOCKS = 4
FFN_STEPS = 4
GROUP = QUERY_HEADS // KEY_VALUE_HEADS
UNSEEN = -1e30
EXPONENT = math.log2(math.e) / math.sqrt(HEAD_SIZE)
LANES = 128
CAUSAL_FLOPS = 20 * 10**9
NT = (((1,), (1,)), ((), ()))


def to_next(value):
    count = lax.axis_size("blk")
    return lax.ppermute(value, "blk", [(i, (i + 1) % count) for i in range(count)])


def to_previous(value):
    count = lax.axis_size("blk")
    return lax.ppermute(value, "blk", [(i, (i - 1) % count) for i in range(count)])


def after(value, done):
    return lax.optimization_barrier((value, done))[0]


def attend_kernel(back, last, *refs):
    if back == 0:
        q_ref, k_ref, v_ref, position_ref, causal_ref = refs[:5]
        *out, bias_ref = refs[5:]
    else:
        q_ref, k_ref, v_ref, position_ref, stat_ref, sum_ref = refs[:6]
        if last:
            residual_ref, gain_ref, attended_out, normed_ref, bias_ref, attended_ref, semaphores = refs[6:]
        else:
            *out, bias_ref = refs[6:]

    def attended_copy(index):
        wide = GROUP * HEAD_SIZE
        columns = pl.ds(pl.multiple_of(index * wide, wide), wide)
        return pltpu.make_async_copy(attended_ref.at[:, columns], attended_out.at[:, columns], semaphores.at[index])

    rows = q_ref.shape[0]
    key = lax.broadcasted_iota(jnp.int32, (rows, rows), 0) - back * rows
    query = lax.broadcasted_iota(jnp.int32, (rows, rows), 1)
    seen = key >= query - position_ref[...]
    bias_ref[...] = jnp.where(seen, causal_ref[...] if back == 0 else 0.0, UNSEEN)

    def group(index, _):
        group_columns = pl.ds(pl.multiple_of(index * HEAD_SIZE, HEAD_SIZE), HEAD_SIZE)
        keys = k_ref[:, group_columns]
        values = v_ref[:, group_columns].T
        for head in range(GROUP):
            columns = pl.ds(pl.multiple_of((index * GROUP + head) * HEAD_SIZE, HEAD_SIZE), HEAD_SIZE)
            features = slice(head * HEAD_SIZE, (head + 1) * HEAD_SIZE)
            for start in range(0, rows, LANES):
                some = slice(start, start + LANES)
                scores = lax.dot_general(
                    keys, q_ref[some, columns], NT, preferred_element_type=jnp.float32
                )
                scores = scores + bias_ref[:, some]
                top = jnp.max(scores, axis=0, keepdims=True)
                if back > 0:
                    top_before = stat_ref[index, head : head + 1, some]
                    top = jnp.maximum(top, top_before)
                weights = jnp.exp2((scores - top) * EXPONENT)
                total = jnp.sum(weights, axis=0, keepdims=True)
                mixed = jnp.dot(values, weights.astype(jnp.bfloat16), preferred_element_type=jnp.float32)
                if back > 0:
                    shrink = jnp.exp2((top_before - top) * EXPONENT)
                    total = total + stat_ref[index, GROUP + head : GROUP + head + 1, some] * shrink
                    mixed = mixed + sum_ref[index, features, some] * shrink
                if last:
                    attended_ref[some, columns] = (mixed * (1.0 / total)).T.astype(jnp.bfloat16)
                else:
                    out[0][index, head : head + 1, some] = top
                    out[0][index, GROUP + head : GROUP + head + 1, some] = total
                    out[1][index, features, some] = mixed
        if last:
            attended_copy(index).start()
        return 0

    lax.fori_loop(0, KEY_VALUE_HEADS, group, 0, unroll=True)
    if last:
        normed_rows(attended_ref, residual_ref, gain_ref, normed_ref)
        for index in range(KEY_VALUE_HEADS):
            attended_copy(index).wait()


def attend(back, last, queries, keys, values, positions, carry=()):
    rows = queries.shape[0]
    out_specs = None
    if last:
        out_shape = (jax.ShapeDtypeStruct(queries.shape, jnp.bfloat16),) * 2
        out_specs = (pl.BlockSpec(memory_space=pltpu.HBM), pl.BlockSpec(memory_space=pltpu.VMEM))
    else:
        out_shape = (
            jax.ShapeDtypeStruct((KEY_VALUE_HEADS, 2 * GROUP, rows), jnp.float32),
            jax.ShapeDtypeStruct((KEY_VALUE_HEADS, GROUP * HEAD_SIZE, rows), jnp.float32),
        )
    scratch_shapes = [pltpu.VMEM((rows, rows), jnp.float32)]
    in_specs = [pl.BlockSpec(memory_space=pltpu.VMEM)] * (4 + len(carry))
    if last:
        scratch_shapes += [
            pltpu.VMEM(queries.shape, jnp.bfloat16),
            pltpu.SemaphoreType.DMA((KEY_VALUE_HEADS,)),
        ]
    if out_specs is None:
        out_specs = (pl.BlockSpec(memory_space=pltpu.VMEM),) * len(out_shape)
    return pl.pallas_call(
        functools.partial(attend_kernel, back, last),
        out_shape=out_shape,
        in_specs=in_specs,
        out_specs=out_specs,
        scratch_shapes=scratch_shapes,
        name=f"attend_{back}",
        compiler_params=pltpu.CompilerParams(vmem_limit_bytes=16 << 20),
        cost_estimate=pl.CostEstimate(
            flops=4 * QUERY_HEADS * rows * rows * HEAD_SIZE,
            transcendentals=QUERY_HEADS * rows * rows,
            bytes_accessed=12 << 20,
        ),
    )(queries, keys, values, positions, *carry)


def weigh_kernel(back, q_ref, k_ref, position_ref, stat_ref, weights_out, stat_out, bias_ref):
    rows = q_ref.shape[0]
    key = lax.broadcasted_iota(jnp.int32, (rows, rows), 0) - back * rows
    query = lax.broadcasted_iota(jnp.int32, (rows, rows), 1)
    bias_ref[...] = jnp.where(key >= query - position_ref[...], 0.0, UNSEEN)

    def group(index, _):
        keys = k_ref[:, pl.ds(pl.multiple_of(index * HEAD_SIZE, HEAD_SIZE), HEAD_SIZE)]
        for head in range(GROUP):
            columns = pl.ds(pl.multiple_of((index * GROUP + head) * HEAD_SIZE, HEAD_SIZE), HEAD_SIZE)
            for start in range(0, rows, LANES):
                some = slice(start, start + LANES)
                scores = lax.dot_general(
                    keys, q_ref[some, columns], NT, preferred_element_type=jnp.float32
                )
                scores = scores + bias_ref[:, some]
                top_before = stat_ref[index, head : head + 1, some]
                top = jnp.maximum(jnp.max(scores, axis=0, keepdims=True), top_before)
                weights = jnp.exp2((scores - top) * EXPONENT)
                shrink = jnp.exp2((top_before - top) * EXPONENT)
                total = jnp.sum(weights, axis=0, keepdims=True)
                total = total + stat_ref[index, GROUP + head : GROUP + head + 1, some] * shrink
                weights_out[index, head * rows : (head + 1) * rows, some] = weights.astype(jnp.bfloat16)
                stat_out[index, head : head + 1, some] = shrink / total
                stat_out[index, GROUP + head : GROUP + head + 1, some] = 1.0 / total
        return 0

    lax.fori_loop(0, KEY_VALUE_HEADS, group, 0, unroll=True)


def weigh(back, queries, keys, positions, stat):
    rows = queries.shape[0]
    return pl.pallas_call(
        functools.partial(weigh_kernel, back),
        out_shape=(
            jax.ShapeDtypeStruct((KEY_VALUE_HEADS, GROUP * rows, rows), jnp.bfloat16),
            jax.ShapeDtypeStruct(stat.shape, jnp.float32),
        ),
        scratch_shapes=[pltpu.VMEM((rows, rows), jnp.float32)],
        name=f"weigh_{back}",
        compiler_params=pltpu.CompilerParams(vmem_limit_bytes=16 << 20),
        cost_estimate=pl.CostEstimate(
            flops=2 * QUERY_HEADS * rows * rows * HEAD_SIZE,
            transcendentals=QUERY_HEADS * rows * rows,
            bytes_accessed=8 << 20,
        ),
    )(queries, keys, positions, stat)


def mix_kernel(v_ref, weights_ref, stat_ref, sum_ref, residual_ref, gain_ref, attended_out, normed_ref, attended_ref, semaphores):
    rows = v_ref.shape[0]
    wide = GROUP * HEAD_SIZE

    def attended_copy(index):
        columns = pl.ds(pl.multiple_of(index * wide, wide), wide)
        return pltpu.make_async_copy(attended_ref.at[:, columns], attended_out.at[:, columns], semaphores.at[index])

    def group(index, _):
        values = v_ref[:, pl.ds(pl.multiple_of(index * HEAD_SIZE, HEAD_SIZE), HEAD_SIZE)].T
        for head in range(GROUP):
            columns = pl.ds(pl.multiple_of((index * GROUP + head) * HEAD_SIZE, HEAD_SIZE), HEAD_SIZE)
            features = slice(head * HEAD_SIZE, (head + 1) * HEAD_SIZE)
            for start in range(0, rows, LANES):
                some = slice(start, start + LANES)
                mixed = jnp.dot(
                    values,
                    weights_ref[index, head * rows : (head + 1) * rows, some],
                    preferred_element_type=jnp.float32,
                )
                mixed = mixed * stat_ref[index, GROUP + head : GROUP + head + 1, some]
                mixed = mixed + sum_ref[index, features, some] * stat_ref[index, head : head + 1, some]
                attended_ref[some, columns] = mixed.T.astype(jnp.bfloat16)
        attended_copy(index).start()
        return 0

    lax.fori_loop(0, KEY_VALUE_HEADS, group, 0, unroll=4)
    normed_rows(attended_ref, residual_ref, gain_ref, normed_ref)
    for index in range(KEY_VALUE_HEADS):
        attended_copy(index).wait()


def mix(values, weights, stat, sums, residual, gain):
    return pl.pallas_call(
        mix_kernel,
        out_shape=(jax.ShapeDtypeStruct(residual.shape, jnp.bfloat16),) * 2,
        out_specs=(pl.BlockSpec(memory_space=pltpu.HBM), pl.BlockSpec(memory_space=pltpu.VMEM)),
        scratch_shapes=[
            pltpu.VMEM(residual.shape, jnp.bfloat16),
            pltpu.SemaphoreType.DMA((KEY_VALUE_HEADS,)),
        ],
        name="mix",
        compiler_params=pltpu.CompilerParams(vmem_limit_bytes=16 << 20),
        cost_estimate=pl.CostEstimate(
            flops=2 * weights.size * HEAD_SIZE, transcendentals=0, bytes_accessed=12 << 20
        ),
    )(values, weights, stat, sums, residual, gain)


def causal_kernel(out_ref):
    key = lax.broadcasted_iota(jnp.int32, out_ref.shape, 0)
    query = lax.broadcasted_iota(jnp.int32, out_ref.shape, 1)
    out_ref[...] = jnp.where(key <= query, 0.0, UNSEEN)


def causal_bias(rows):
    return pl.pallas_call(
        causal_kernel,
        out_shape=jax.ShapeDtypeStruct((rows, rows), jnp.float32),
        name="causal",
        compiler_params=pltpu.CompilerParams(vmem_limit_bytes=4 << 20),
        cost_estimate=pl.CostEstimate(flops=CAUSAL_FLOPS, transcendentals=0, bytes_accessed=rows * rows * 4),
    )()


def normed_rows(attended_ref, residual_ref, gain_ref, out_ref):
    step = 16

    def some(index, _):
        rows = pl.ds(pl.multiple_of(index * step, step), step)
        stream = residual_ref[rows, :].astype(jnp.float32) + attended_ref[rows, :].astype(jnp.float32)
        mean = jnp.mean(stream * stream, axis=-1, keepdims=True)
        out_ref[rows, :] = (stream * lax.rsqrt(mean + 1e-05) * gain_ref[...]).astype(jnp.bfloat16)
        return 0

    lax.fori_loop(0, out_ref.shape[0] // step, some, 0, unroll=2)


def gate_kernel(shards, slot, *refs):
    normed_ref = refs[0]
    weights = refs[1 : 1 + 2 * shards]
    out_ref, lhs_ref = refs[1 + 2 * shards :]
    units = weights[0].shape[0]
    for index, weight in enumerate(weights):
        lhs_ref[index * slot : index * slot + units, :] = weight[...]
        lhs_ref[index * slot + units : (index + 1) * slot, :] = jnp.zeros((slot - units, lhs_ref.shape[1]), lhs_ref.dtype)
    both = lax.dot_general(lhs_ref[...], normed_ref[...], NT, preferred_element_type=jnp.float32)
    for shard in range(shards):
        gate = both[2 * shard * slot : (2 * shard + 1) * slot]
        up = both[(2 * shard + 1) * slot : (2 * shard + 2) * slot]
        out_ref[shard * slot : (shard + 1) * slot, :] = (jax.nn.silu(gate) * up).astype(jnp.bfloat16)


def down_kernel(slot, *refs):
    hidden_ref = refs[0]
    downs = refs[1 : 1 + FFN_STEPS]
    out_ref, rhs_ref, piece_ref, semaphores = refs[1 + FFN_STEPS :]
    units = downs[0].shape[0]
    for index, rows in enumerate(downs):
        rhs_ref[index * slot : index * slot + units, :] = rows[...]
        rhs_ref[index * slot + units : (index + 1) * slot, :] = jnp.zeros((slot - units, rhs_ref.shape[1]), rhs_ref.dtype)
    hidden = hidden_ref[...].T
    width = out_ref.shape[1] // semaphores.shape[0]
    copies = []
    for piece in range(semaphores.shape[0]):
        some = slice(piece * width, (piece + 1) * width)
        piece_ref[:, some] = jnp.dot(hidden, rhs_ref[:, some], preferred_element_type=jnp.float32).astype(jnp.bfloat16)
        copies.append(pltpu.make_async_copy(piece_ref.at[:, some], out_ref.at[:, some], semaphores.at[piece]))
        copies[-1].start()
    for copy in copies:
        copy.wait()


def gate_up(normed, *weights):
    rows, features = normed.shape
    shards = len(weights) // 2
    units = weights[0].shape[0]
    slot = -(-units // 16) * 16
    return pl.pallas_call(
        functools.partial(gate_kernel, shards, slot),
        out_shape=jax.ShapeDtypeStruct((shards * slot, rows), jnp.bfloat16),
        scratch_shapes=[pltpu.VMEM((2 * shards * slot, features), jnp.bfloat16)],
        name=f"gate_up_{shards}",
        compiler_params=pltpu.CompilerParams(vmem_limit_bytes=16 << 20),
        cost_estimate=pl.CostEstimate(
            flops=4 * shards * rows * features * units,
            transcendentals=shards * rows * units,
            bytes_accessed=2 * shards * units * features * 2 + rows * features * 2,
        ),
    )(normed, *weights)


def down(hidden, downs):
    units, features = downs[0].shape
    rows = hidden.shape[1]
    slot = hidden.shape[0] // FFN_STEPS
    return pl.pallas_call(
        functools.partial(down_kernel, slot),
        out_shape=jax.ShapeDtypeStruct((rows, features), jnp.bfloat16),
        out_specs=pl.BlockSpec(memory_space=pltpu.HBM),
        scratch_shapes=[
            pltpu.VMEM((FFN_STEPS * slot, features), jnp.bfloat16),
            pltpu.VMEM((rows, features), jnp.bfloat16),
            pltpu.SemaphoreType.DMA((8,)),
        ],
        name="down",
        compiler_params=pltpu.CompilerParams(vmem_limit_bytes=16 << 20),
        cost_estimate=pl.CostEstimate(
            flops=64 * 2 * FFN_STEPS * rows * features * units,
            transcendentals=0,
            bytes_accessed=4 << 20,
        ),
    )(hidden, *downs)


def per_device(
    query_states,
    rotated_key_state,
    value_state_rows,
    positions,
    residual,
    norm_gain,
    gate_weight,
    up_weight,
    down_weight,
):
    positions = positions[None, :]
    keys = [rotated_key_state]
    values = [value_state_rows]
    gates, ups, downs = [gate_weight], [up_weight], [down_weight]
    causal = causal_bias(query_states.shape[0])
    gates.append(to_previous(after(gates[0], causal)))
    ups.append(to_previous(after(ups[0], causal)))
    downs.append(to_previous(after(downs[0], causal)))
    keys.append(to_next(after(keys[0], causal)))
    values.append(to_next(after(values[0], causal)))

    carry = attend(0, False, query_states, keys[0], values[0], positions, (causal,))
    keys.append(to_next(after(keys[1], carry[0])))
    gates.append(to_previous(after(gates[1], carry[0])))
    values.append(to_next(after(values[1], carry[0])))
    ups.append(to_previous(after(ups[1], carry[0])))

    carry = attend(1, False, query_states, keys[1], values[1], positions, carry)
    downs.append(to_previous(after(downs[1], carry[0])))
    keys.append(to_next(after(keys[2], carry[0])))
    gates.append(to_previous(after(gates[2], carry[0])))
    values.append(to_next(after(values[2], carry[0])))

    carry = attend(2, False, query_states, keys[2], values[2], positions, carry)
    ups.append(to_previous(after(ups[2], carry[0])))
    downs.append(to_previous(after(downs[2], carry[0])))

    weights, scales = weigh(3, query_states, keys[3], positions, carry[0])
    attended, normed = mix(values[3], weights, scales, carry[1], residual, norm_gain[None, :])
    units = gate_up(normed, *[rows for pair in zip(gates, ups) for rows in pair])
    ffn_part = down(units, downs)
    return (attended, ffn_part)


def solution(mesh):
    rows = P("blk", None)
    in_specs = (rows, rows, rows, P("blk"), rows, P(), rows, rows, rows)
    return jax.shard_map(
        per_device, mesh=mesh, in_specs=in_specs, out_specs=(rows, rows), check_vma=False
    )
```
